32 devices in a mesh: ep: 16 (over z, x, core), es: 2 (over y).
Axes of the slice: x: 2, y: 2, z: 4, core: 2. Of those that a mesh axis runs over, the one named last changes fastest.
Arguments:
- inputs: bfloat16 [16384, 1024], P(('ep', 'es')), may hold values from -6 to 6
- grad_output: bfloat16 [16384, 1024], P(('ep', 'es')), may hold values from -6 to 6
- expert_choice: int32 [16384, 1], P(('ep', 'es')), may hold values from 0 to 15; in each aligned block of 512 rows (0 to 511, 512 to 1023, ...) at most 45 rows name the same one
- pre_gain: float32 [1024], replicated, may hold values from 0.25 to 1.75
- pre_shift: float32 [1024], replicated, may hold values from -4 to 4
- w_query: bfloat16 [1024, 1024], P('es'), may hold values from -0.1875 to 0.1875
- w_key: bfloat16 [1024, 1024], P('es'), may hold values from -0.1875 to 0.1875
- w_value: bfloat16 [1024, 1024], P('es'), may hold values from -0.1875 to 0.1875
- w_output: bfloat16 [1024, 1024], P('es'), may hold values from -3 to 3
- mid_gain: float32 [1024], replicated, may hold values from 0.25 to 1.75
- mid_shift: float32 [1024], replicated, may hold values from -4 to 4
- w_up: bfloat16 [1024, 4096], P('es'), may hold values from -0.1875 to 0.1875
- w_down: bfloat16 [4096, 1024], P('es'), may hold values from -0.09375 to 0.09375
- w_router: bfloat16 [1024, 16], replicated, may hold values from -0.3125 to 0.3125
- w_mix: bfloat16 [1024, 2], replicated, may hold values from -0.3125 to 0.3125
- expert_up: bfloat16 [16, 1024, 4096], P('ep', None, 'es'), may hold values from -0.1875 to 0.1875
- expert_down: bfloat16 [16, 4096, 1024], P('ep', 'es'), may hold values from -6 to 6
Outputs:
- output: bfloat16 [16384, 1024], P(('ep', 'es'))
- grad_inputs: float32 [16384, 1024], P(('ep', 'es'))
- grad_pre_gain: float32 [1024], P(('ep', 'es'))
- grad_pre_shift: float32 [1024], P(('ep', 'es'))
- grad_w_query: float32 [1024, 1024], P(('ep', 'es'))
- grad_w_key: float32 [1024, 1024], P(('ep', 'es'))
- grad_w_value: float32 [1024, 1024], P(('ep', 'es'))
- grad_w_output: float32 [1024, 1024], P(('ep', 'es'))
- grad_mid_gain: float32 [1024], P(('ep', 'es'))
- grad_mid_shift: float32 [1024], P(('ep', 'es'))
- grad_w_up: float32 [1024, 4096], P(('ep', 'es'))
- grad_w_down: float32 [4096, 1024], P(('ep', 'es'))
- grad_w_router: float32 [1024, 16], P(('ep', 'es'))
- grad_w_mix: float32 [1024, 2], P(('ep', 'es'))
- grad_expert_up: float32 [16, 1024, 4096], P('ep', None, 'es')
- grad_expert_down: float32 [16, 4096, 1024], P('ep', 'es')
The draws below stay inside these ranges and needn't reach their ends.
Inputs may be any that keep to these rules, and one draw needn't show every extreme that they name: `expert_choice`: in each aligned block of 512 rows (the rows of one device) no expert is named more than 45 times; in some of these blocks an expert is named exactly 45 times.
All inputs are finite; a program needn't handle non-finite values.
Results may differ from the reference program's by a relative error of at most 0.019.
The reference program's roundings to bfloat16 on the way count: a program that leaves them out, or rounds other values in their place, can miss the bound.
Values may be sent and summed in bfloat16 or wider, within the bound.
No kernel may reach another device: no remote copies, remote signals or barrier semaphores. Data moves between devices by JAX's collectives and lax.ppermute only.
A program may use at most 320 MiB of HBM per device.

```python
import math
import jax
import jax.numpy as jnp
import numpy as np
from jax import lax

D = 1024
HEADS = 16
HEAD_DIM = 64
FF = 4096
TOK_DEV = 512
EXPERTS = 16
SEQ = 1024
TOKENS = 16384
CAP = 45


def spiked(values, key, source, target, shards_of, factor):
    owner, partner = [(jnp.arange(values.shape[dim]) // (values.shape[dim] // shards_of)).reshape([-1 if axis == dim else 1 for axis in range(values.ndim)]) for dim in (source, target)]
    chosen = jax.random.permutation(key, shards_of)[partner]
    strong = (owner == chosen) | (owner == (partner + shards_of // 2) % shards_of)
    return jnp.where(strong, factor * values, values)


def levels(rng, extent, cuts, smallest, largest):
    loudness, own = 1.0, jax.random.fold_in(rng, 6)
    for axis_at, blocks in cuts:
        heights = jnp.exp(jax.random.uniform(jax.random.fold_in(own, axis_at), (blocks,), jnp.float32, smallest / len(cuts), largest / len(cuts)))
        loudness = loudness * jnp.repeat(heights, extent[axis_at] // blocks).reshape([-1 if axis == axis_at else 1 for axis in range(len(extent))])
    return loudness


def assign_block(rng, own, number, rows, number_of, top, limit, lean):
    ranking = jax.random.permutation(rng, number_of)
    crowded, ordinary = load_shares(number_of, rows * top, limit, lean, True), load_shares(number_of, rows * top, limit, lean, False)
    places = jnp.arange(number_of)

    def named(lengths, offset_by):
        used = int((lengths > 0).sum())
        fixed = max(1, used // 4)
        passed = fixed + (places - fixed + offset_by * (used - fixed)) % max(1, number_of - fixed)
        return jnp.zeros((number_of,), jnp.int32).at[ranking[jnp.where(places < fixed, places, passed)]].set(jnp.asarray(lengths, jnp.int32))

    lengths = jnp.where(number % 4 == 0, named(crowded, number // 4), named(ordinary, number - number // 4 - 1))
    mixed = jax.random.permutation(jax.random.fold_in(own, 3), number_of)
    donor, sink = mixed[0:number_of // 2 * 2:2], mixed[1:number_of // 2 * 2:2]
    room = jnp.minimum(lengths[donor] - 1, limit - lengths[sink]) // 2
    room = jnp.where((donor == ranking[0]) | (sink == ranking[0]) | (lengths[sink] == 0), 0, jnp.maximum(room, 0))
    passed = jax.random.randint(jax.random.fold_in(own, 4), (number_of // 2,), 0, 1 << 20) % (room + 1)
    lengths = lengths.at[donor].add(-passed).at[sink].add(passed)
    items = jnp.searchsorted(jnp.cumsum(lengths), jnp.arange(rows * top), side="right").astype(jnp.int32)
    grid = items.reshape(top, rows).T
    grid = grid[jax.random.permutation(jax.random.fold_in(own, 1), rows)]
    offset_by = jax.random.randint(jax.random.fold_in(own, 2), (rows, 1), 0, top)
    return jnp.take_along_axis(grid, (jnp.arange(top)[None, :] + offset_by) % top, axis=1)


def load_shares(count, total, reach, skew, full):
    portions = [(1 << 20) // math.isqrt(grade ** skew) + 1 for grade in range(1, count + 1)]
    largest = reach if full else min(reach, max(-(-total // count), total * portions[0] // sum(portions)))
    least = 1 if total - largest >= count - 1 else 0
    counts, surplus = [largest] + [least] * (count - 1), total - largest - least * (count - 1)
    while surplus > 0:
        candidates = [i for i in range(1, count) if counts[i] < largest] or [i for i in range(1, count) if counts[i] < reach]
        pool, budget = sum([portions[i] for i in candidates]), surplus
        for i in candidates:
            more = min(reach - counts[i], max(1, budget * portions[i] // pool), surplus)
            counts[i] = counts[i] + more
            surplus = surplus - more
    return np.array(counts)


def noise(own_key, extent, width, limit, cuts=(), kind=jnp.bfloat16):
    drawn = jax.random.normal(own_key, extent, jnp.float32) * width
    if len(cuts) > 0:
        drawn = levels(own_key, extent, cuts, -0.22, 0.18) * drawn
    return jnp.clip(drawn, min=-limit, max=limit).astype(kind)


def noise_with(key, shape, scale, reach, pieces, heavy, held_as=jnp.bfloat16):
    drawn = scale * jax.random.normal(key, shape, jnp.float32)
    if pieces:
        drawn = drawn * levels(key, shape, pieces, -0.22, 0.18)
    return jnp.clip(spiked(drawn, jax.random.fold_in(key, 3), *heavy), -reach, reach).astype(held_as)


def setup_inputs(seed: int = 0) -> dict:
    key_list = jax.random.split(jax.random.key(seed), 18)
    inputs = noise(key_list[0], (TOKENS, D), 1.0, 6.0, ((0, 32),))
    grad_output = noise_with(key_list[1], (TOKENS, D), 1.0, 6.0, ((0, 32),), (0, 1, 32, 2.75))
    expert_choice_keys = jax.random.split(jax.random.fold_in(key_list[2], 1), TOKENS // TOK_DEV)
    expert_choice_turns = jax.random.permutation(jax.random.fold_in(key_list[2], 3), TOKENS // TOK_DEV)
    expert_choice = jax.vmap(lambda own, number: assign_block(jax.random.fold_in(key_list[2], 2), own, number, TOK_DEV, EXPERTS, 1, CAP, 1))(expert_choice_keys, expert_choice_turns).reshape((TOKENS, 1))
    pre_gain = jnp.clip(1.0 + 0.15 * jax.random.normal(key_list[3], (D,), jnp.float32), 0.25, 1.75)
    pre_shift = noise(key_list[4], (D,), 0.3, 4.0, (), jnp.float32)
    w_query = noise(key_list[5], (D, D), D ** -0.5, 0.1875, ((0, 2),))
    w_key = noise(key_list[6], (D, D), D ** -0.5, 0.1875, ((0, 2),))
    w_value = noise(key_list[7], (D, D), D ** -0.5, 0.1875, ((0, 2),))
    w_output = noise(key_list[8], (D, D), (2 * D // TOK_DEV) ** -0.5, 3.0, ((0, 2),))
    mid_gain = jnp.clip(1.0 + 0.15 * jax.random.normal(key_list[9], (D,), jnp.float32), 0.25, 1.75)
    mid_shift = noise(key_list[10], (D,), 0.3, 4.0, (), jnp.float32)
    w_up = noise(key_list[11], (D, FF), D ** -0.5, 0.1875, ((0, 2),))
    w_down = noise(key_list[12], (FF, D), FF ** -0.5, 0.09375, ((0, 2),))
    w_router = noise(key_list[13], (D, EXPERTS), (0.7 * D ** -0.5), 0.3125)
    w_mix = noise(key_list[14], (D, 2), (0.7 * D ** -0.5), 0.3125)
    expert_up = noise(key_list[15], (EXPERTS, D, FF), D ** -0.5, 0.1875, ((0, 16), (2, 2)))
    expert_down = noise(key_list[16], (EXPERTS, FF, D), (2.0 * EXPERTS * FF ** -0.5), 6.0, ((0, 16), (1, 2)))
    return {"inputs": inputs, "grad_output": grad_output, "expert_choice": expert_choice, "pre_gain": pre_gain, "pre_shift": pre_shift, "w_query": w_query, "w_key": w_key, "w_value": w_value, "w_output": w_output, "mid_gain": mid_gain, "mid_shift": mid_shift, "w_up": w_up, "w_down": w_down, "w_router": w_router, "w_mix": w_mix, "expert_up": expert_up, "expert_down": expert_down}


@jax.custom_vjp
def low(v):
    return lax.optimization_barrier(v.astype(jnp.bfloat16)).astype(jnp.float32)

@jax.custom_vjp
def low_back(v):
    return v

def low_keep(v):
    return (low(v), None)

def low_pass(kept, grad):
    return (grad,)

def back_keep(v):
    return (v, None)

def back_low(kept, grad):
    return (low(grad),)
low.defvjp(low_keep, low_pass)
low_back.defvjp(back_keep, back_low)

def matmul(left, right):
    return jnp.dot(left, right, precision=lax.Precision.HIGHEST, preferred_element_type=jnp.float32)

def layer_norm(values, gain, shift):
    center = lax.optimization_barrier(jnp.mean(values, axis=-1, keepdims=True))
    centred = values - center
    spread = lax.optimization_barrier(jnp.mean(centred * centred, axis=-1, keepdims=True))
    return centred * lax.rsqrt(spread + 1e-05) * gain + shift

def gelu_tanh(values):
    return jax.nn.gelu(values, approximate=True)

def attend_sequence(block):
    query, keys, values = block
    scores = jnp.einsum('qhd,khd->hqk', query, keys, precision=lax.Precision.HIGHEST)
    scores = low_back(scores * HEAD_DIM ** (-0.5))
    positions = jnp.arange(SEQ, dtype=jnp.int32)
    causal = positions[:, None] >= positions[None, :]
    scores = jnp.where(causal[None], scores, -1e+30)
    probs = low(jax.nn.softmax(scores, axis=-1))
    return jnp.einsum('hqk,khd->qhd', probs, values, precision=lax.Precision.HIGHEST)

def run_expert(block):
    rows, up_weight, down_weight = block
    expert_pre = low_back(matmul(rows, up_weight))
    expert_hidden = low(gelu_tanh(expert_pre))
    return matmul(expert_hidden, down_weight)

def reference(inputs, grad_output, expert_choice, pre_gain, pre_shift, w_query, w_key, w_value, w_output, mid_gain, mid_shift, w_up, w_down, w_router, w_mix, expert_up, expert_down):
    devices = TOKENS // TOK_DEV
    slots_all = devices * CAP
    chosen = expert_choice[:, 0]
    onehot = (chosen[:, None] == jnp.arange(EXPERTS, dtype=jnp.int32)[None, :]).astype(jnp.int32)
    running = jnp.cumsum(onehot.reshape(devices, TOK_DEV, EXPERTS), axis=1).reshape(TOKENS, EXPERTS)
    ranks = lax.optimization_barrier(jnp.sum(onehot * running, axis=1)) - 1
    owner = jnp.arange(TOKENS, dtype=jnp.int32) // TOK_DEV
    place = (owner * CAP + ranks).astype(jnp.int32)

    def forward(params):
        source, gain_a, shift_a, query_w, key_w, value_w, output_w, gain_b, shift_b, up_w, down_w, router_w, mix_w, expert_up_w, expert_down_w = params
        first = low(layer_norm(source, gain_a, shift_a))
        query = low(low_back(matmul(first, query_w)))
        keys = low(low_back(matmul(first, key_w)))
        values = low(low_back(matmul(first, value_w)))

        def shaped(array):
            return array.reshape(TOKENS // SEQ, SEQ, HEADS, HEAD_DIM)
        attended = lax.map(jax.checkpoint(attend_sequence), (shaped(query), shaped(keys), shaped(values)))
        attended = low(low_back(attended.reshape(TOKENS, D)))
        resid = source + low_back(matmul(attended, output_w))
        second = low(layer_norm(resid, gain_b, shift_b))
        hidden = low(gelu_tanh(low_back(matmul(second, up_w))))
        dense = low_back(matmul(hidden, down_w))
        route_probs = jax.nn.softmax(low_back(matmul(second, router_w)), axis=-1)
        gate = jnp.take_along_axis(route_probs, expert_choice, axis=1)
        mix = jax.nn.softmax(low_back(matmul(second, mix_w)), axis=-1)
        buffer = jnp.zeros((EXPERTS, slots_all, D), jnp.float32).at[chosen, place].set(second)
        expert_out = lax.map(jax.checkpoint(run_expert), (buffer, expert_up_w, expert_down_w))
        expert_out = low(low_back(expert_out))
        routed = expert_out[chosen, place]
        return resid + mix[:, 0:1] * dense + mix[:, 1:2] * gate * routed
    params = tuple((a.astype(jnp.float32) for a in (inputs, pre_gain, pre_shift, w_query, w_key, w_value, w_output, mid_gain, mid_shift, w_up, w_down, w_router, w_mix, expert_up, expert_down)))
    result, pullback = jax.vjp(forward, params)
    grads = pullback(grad_output.astype(jnp.float32))[0]
    return (result.astype(jnp.bfloat16), grads[0], grads[1], grads[2], grads[3], grads[4], grads[5], grads[6], grads[7], grads[8], grads[9], grads[10], grads[11], grads[12], grads[13], grads[14])
```

```python
import jax
import jax.numpy as jnp
from jax import lax
from jax.experimental import pallas as pl
from jax.experimental.pallas import tpu as pltpu
from jax.sharding import PartitionSpec as P

HEAD_DIM = 64
SCALE = HEAD_DIM ** (-0.5)
LANES = 128
QB = 256
BF = jnp.bfloat16
F32 = jnp.float32


def layer_norm(values, gain, shift):
    center = jnp.mean(values, axis=-1, keepdims=True)
    centred = values - center
    spread = jnp.mean(centred * centred, axis=-1, keepdims=True)
    return centred * lax.rsqrt(spread + 1e-05) * gain + shift


def gelu_tanh(values):
    return jax.nn.gelu(values, approximate=True)


def matmul(left, right):
    return jnp.dot(left, right, preferred_element_type=F32)


def matmul_nt(left, right):
    return lax.dot_general(left, right, (((1,), (1,)), ((), ())), preferred_element_type=F32)


def matmul_tn(left, right):
    return lax.dot_general(left, right, (((0,), (0,)), ((), ())), preferred_element_type=F32)


def swap(value):
    return lax.ppermute(value, "es", [(0, 1), (1, 0)])


def core_swap(value):
    size = lax.axis_size("ep")
    return lax.ppermute(value, "ep", [(i, i ^ 1) for i in range(size)])


def rows_of(value, start, count, axis=0):
    return lax.dynamic_slice_in_dim(value, start, count, axis)


def fetch(payload, core):
    half = payload.shape[0] // 2
    got = swap(rows_of(payload, core * half, half))
    other = core_swap(got)
    first = core == 0
    return jnp.concatenate([jnp.where(first, got, other), jnp.where(first, other, got)], 0)


def ordered(own, other, side, axis=0):
    early = side == 0
    return jnp.concatenate(
        [jnp.where(early, own, other), jnp.where(early, other, own)], axis
    )


def head_masks():
    lane = lax.broadcasted_iota(jnp.int32, (1, LANES), 1)
    return (lane < HEAD_DIM, lane >= HEAD_DIM)


def attend_kernel(qkv_ref, out_ref, lse_ref):
    length = qkv_ref.shape[0]
    masks = head_masks()
    for start in range(0, length, QB):
        reach = start + QB
        query = qkv_ref[start:reach, 0:LANES] * SCALE
        keys = qkv_ref[0:reach, LANES : 2 * LANES]
        values = qkv_ref[0:reach, 2 * LANES :]
        row = lax.broadcasted_iota(jnp.int32, (QB, reach), 0) + start
        col = lax.broadcasted_iota(jnp.int32, (QB, reach), 1)
        outs, logs = [], []
        for mask in masks:
            scores = matmul_nt(jnp.where(mask, query, 0.0).astype(BF), keys)
            scores = jnp.where(col <= row, scores, -1e30)
            peak = jnp.max(scores, axis=-1, keepdims=True)
            expo = jnp.exp(scores - peak)
            total = jnp.sum(expo, axis=-1, keepdims=True)
            probs = (expo * (1.0 / total)).astype(BF)
            outs.append(matmul(probs, values))
            logs.append(peak + jnp.log(total))
        out_ref[start:reach, :] = jnp.where(masks[0], outs[0], outs[1]).astype(BF)
        lse_ref[start:reach, :] = jnp.where(masks[0], logs[0], logs[1])


def attend_back_kernel(qkv_ref, out_ref, lse_ref, grad_ref, dqkv_ref, dk_ref, dv_ref):
    length = qkv_ref.shape[0]
    masks = head_masks()
    for start in reversed(range(0, length, QB)):
        reach = start + QB
        query = qkv_ref[start:reach, 0:LANES] * SCALE
        keys = qkv_ref[0:reach, LANES : 2 * LANES]
        values = qkv_ref[0:reach, 2 * LANES :]
        grad = grad_ref[start:reach, :]
        weighed = grad.astype(F32) * out_ref[start:reach, :].astype(F32)
        row = lax.broadcasted_iota(jnp.int32, (QB, reach), 0) + start
        col = lax.broadcasted_iota(jnp.int32, (QB, reach), 1)
        dq, dk, dv = [], None, None
        for h, mask in enumerate(masks):
            q_h = jnp.where(mask, query, 0.0).astype(BF)
            g_h = jnp.where(mask, grad, 0.0).astype(BF)
            scores = matmul_nt(q_h, keys)
            lse = lse_ref[start:reach, h * HEAD_DIM : h * HEAD_DIM + 1]
            probs = jnp.where(col <= row, jnp.exp(scores - lse), 0.0)
            delta = jnp.sum(jnp.where(mask, weighed, 0.0), axis=-1, keepdims=True)
            d_scores = (probs * (matmul_nt(g_h, values) - delta)).astype(BF)
            dq.append(matmul(d_scores, keys))
            dk_h = matmul_tn(d_scores, q_h)
            dv_h = matmul_tn(probs.astype(BF), g_h)
            dk = dk_h if dk is None else dk + dk_h
            dv = dv_h if dv is None else dv + dv_h
        dqkv_ref[start:reach, 0:LANES] = (
            jnp.where(masks[0], dq[0], dq[1]) * SCALE
        ).astype(BF)
        if reach == length:
            dk_ref[...] = dk
            dv_ref[...] = dv
        else:
            dk_ref[0:reach, :] += dk
            dv_ref[0:reach, :] += dv
    dqkv_ref[:, LANES : 2 * LANES] = dk_ref[...].astype(BF)
    dqkv_ref[:, 2 * LANES :] = dv_ref[...].astype(BF)


def attend(qkv):
    length, columns = qkv.shape
    pairs = columns // (3 * LANES)
    wide = pl.BlockSpec((length, 3 * LANES), lambda h: (0, h))
    slim = pl.BlockSpec((length, LANES), lambda h: (0, h))
    return pl.pallas_call(
        attend_kernel,
        grid=(pairs,),
        in_specs=[wide],
        out_specs=[slim, slim],
        out_shape=[
            jax.ShapeDtypeStruct((length, pairs * LANES), BF),
            jax.ShapeDtypeStruct((length, pairs * LANES), F32),
        ],
        name="attend",
    )(qkv)


def attend_back(qkv, out, lse, grad):
    length, columns = qkv.shape
    pairs = columns // (3 * LANES)
    wide = pl.BlockSpec((length, 3 * LANES), lambda h: (0, h))
    slim = pl.BlockSpec((length, LANES), lambda h: (0, h))
    return pl.pallas_call(
        attend_back_kernel,
        grid=(pairs,),
        in_specs=[wide, slim, slim, slim],
        out_specs=wide,
        out_shape=jax.ShapeDtypeStruct((length, columns), BF),
        scratch_shapes=[pltpu.VMEM((length, LANES), F32), pltpu.VMEM((length, LANES), F32)],
        name="attend_back",
    )(qkv, out, lse, grad)


def pieces(value):
    high = lax.reduce_precision(value, 8, 7)
    rest = value - high
    mid = lax.reduce_precision(rest, 8, 7)
    return [high, mid, rest - mid]


def body(
    inputs,
    grad_output,
    expert_choice,
    pre_gain,
    pre_shift,
    w_query,
    w_key,
    w_value,
    w_output,
    mid_gain,
    mid_shift,
    w_up,
    w_down,
    w_router,
    w_mix,
    expert_up,
    expert_down,
):
    tokens, width = inputs.shape
    owners = lax.axis_size("ep")
    experts = w_router.shape[1]
    capacity = max(2, 10 * tokens // (7 * owners))
    room = -(-(capacity + 3) // 16) * 16
    side = lax.axis_index("es")
    rank = lax.axis_index("ep")
    core = rank % 2
    half = w_query.shape[0]
    pairs = half // LANES
    hidden_half = w_down.shape[0]

    def pair_columns(at):
        parts = [
            rows_of(w, at * half, half, 1).reshape(half, pairs, 1, LANES)
            for w in (w_query, w_key, w_value)
        ]
        return jnp.concatenate(parts, 2).reshape(half, 3 * half)

    inputs_other = swap(inputs)
    qkv_other = fetch(pair_columns(1 - side), core)
    grad_other = swap(grad_output)
    choice_other = swap(expert_choice)
    output_other = fetch(w_output, core)
    up_other = fetch(rows_of(w_up, (1 - side) * hidden_half, hidden_half, 1), core)

    source = ordered(inputs, inputs_other, side).astype(F32)
    qkv_w = ordered(pair_columns(side), qkv_other, side)
    up_w = ordered(rows_of(w_up, side * hidden_half, hidden_half, 1), up_other, side)
    upstream = ordered(grad_output, grad_other, side)
    chosen = ordered(expert_choice, choice_other, side)[:, 0]

    onehot = (chosen[:, None] == jnp.arange(experts, dtype=jnp.int32)[None, :]).astype(jnp.int32)
    running = jnp.cumsum(onehot.reshape(2, tokens, experts), axis=1).reshape(2 * tokens, experts)
    place = chosen * room + jnp.sum(onehot * running, axis=1) - 1
    slots = experts * room
    hit = jnp.arange(slots, dtype=jnp.int32)[None, :, None] == place.reshape(2, 1, tokens)
    placing = hit.astype(BF)

    def dispatch(rows):
        return jnp.einsum(
            "bst,btd->bsd", placing, rows.reshape(2, tokens, width), preferred_element_type=F32
        )

    def collect(arrived):
        rows = arrived.reshape(experts, 2, room, width)
        return jnp.einsum(
            "bst,sbd->btd",
            placing,
            rows.transpose(0, 2, 1, 3).reshape(slots, 2, width),
            preferred_element_type=F32,
        ).reshape(2 * tokens, width)

    def exchange(rows):
        return lax.all_to_all(
            rows.reshape(owners, 2 * room, width), "ep", split_axis=0, concat_axis=0, tiled=True
        )

    pad_row = jnp.arange(room, dtype=jnp.int32)[None, None, :, None] - capacity

    def with_scalars(rows, scalars):
        wide = [
            jnp.pad(piece, ((0, 0), (0, 0), (0, width - room)))[:, :, None, :]
            for piece in pieces(scalars)
        ]
        for at, piece in enumerate(wide):
            rows = jnp.where(pad_row == at, piece, rows)
        return rows.astype(BF)

    def scalars_of(rows):
        spare = rows[:, :, capacity : capacity + 3, :room].astype(F32)
        return spare[:, :, 0] + spare[:, :, 1] + spare[:, :, 2]

    def to_owner(rows):
        return rows.reshape(2, owners, room, -1).transpose(1, 0, 2, 3)

    grad_slots = exchange(to_owner(dispatch(upstream)).astype(BF))

    first = layer_norm(source, pre_gain, pre_shift).astype(BF)
    qkv = matmul(first, qkv_w).astype(BF)
    attended, lse = attend(qkv)
    attended_other = swap(attended)
    resid = source + matmul(attended, w_output) + matmul(attended_other, output_other)
    second = layer_norm(resid, mid_gain, mid_shift).astype(BF)
    small_w = jnp.concatenate([w_router, w_mix], 1)
    logits = matmul(second, small_w)
    route_probs = jax.nn.softmax(logits[:, :experts], axis=-1)
    mask = onehot.astype(F32)
    gate = jnp.sum(route_probs * mask, axis=-1, keepdims=True)
    mix = jax.nn.softmax(logits[:, experts:], axis=-1)
    coef = mix[:, 1:2] * gate

    coef_slots = jnp.sum(
        jnp.where(hit, coef.reshape(2, 1, tokens), 0.0), axis=-1
    )
    sent = with_scalars(
        to_owner(dispatch(second)), coef_slots.reshape(2, owners, room).transpose(1, 0, 2)
    )
    arrived = exchange(sent)

    up_pre = matmul(second, up_w)
    hidden = gelu_tanh(up_pre).astype(BF)
    dense = matmul(hidden, w_down)
    up32 = upstream.astype(F32)
    d_dense = (mix[:, 0:1] * up32).astype(BF)
    d_up = jax.vjp(gelu_tanh, up_pre)[1](matmul_nt(d_dense, w_down))[0].astype(BF)
    grad_down = matmul_tn(hidden, d_dense)
    grad_up = matmul_tn(second, d_up)

    count = owners * 2 * room
    coef_there = scalars_of(arrived.reshape(owners, 2, room, width)).reshape(count, 1)
    gathered = arrived.reshape(count, width)
    grad_there = grad_slots.reshape(count, width)
    expert_pre = matmul(gathered, expert_up[0])
    expert_hidden = gelu_tanh(expert_pre).astype(BF)
    expert_out = matmul(expert_hidden, expert_down[0])
    d_routed = (coef_there * grad_there.astype(F32)).astype(BF)
    d_expert_pre = jax.vjp(gelu_tanh, expert_pre)[1](matmul_nt(d_routed, expert_down[0]))[0]
    d_expert_pre = d_expert_pre.astype(BF)
    along = jnp.sum(grad_there.astype(F32) * expert_out, axis=-1)
    d_slots = matmul_nt(d_expert_pre, expert_up[0])
    back = exchange(
        with_scalars(d_slots.reshape(owners, 2, room, width), along.reshape(owners, 2, room))
    )
    out_back = exchange(expert_out.astype(BF))
    grad_expert_down = matmul_tn(expert_hidden, d_routed)[None]
    grad_expert_up = matmul_tn(gathered, d_expert_pre)[None]

    back_rows = back.reshape(owners, 2, room, width)
    along_here = jnp.sum(
        jnp.where(
            hit, scalars_of(back_rows).transpose(1, 0, 2).reshape(2, slots, 1), 0.0
        ),
        axis=1,
    ).reshape(2 * tokens, 1)
    along_dense = jnp.sum(up32 * dense, axis=-1, keepdims=True)
    d_gate = mix[:, 1:2] * along_here
    d_both = jnp.concatenate([along_dense, gate * along_here], 1)
    d_route = route_probs * (mask * d_gate - gate * d_gate)
    d_mix = mix * (d_both - jnp.sum(mix * d_both, axis=-1, keepdims=True))
    d_small = jnp.concatenate([d_route, d_mix], 1).astype(BF)
    grad_small = matmul_tn(second, d_small)

    d_second = matmul_nt(d_up, up_w) + matmul_nt(d_small, small_w) + collect(back)
    theirs = swap(rows_of(d_second, (1 - side) * tokens, tokens).astype(BF))
    d_second = rows_of(d_second, side * tokens, tokens) + theirs.astype(F32)
    d_resid_mid, grad_mid_gain, grad_mid_shift = jax.vjp(
        layer_norm, rows_of(resid, side * tokens, tokens), mid_gain, mid_shift
    )[1](d_second)
    d_resid = grad_output.astype(F32) + d_resid_mid
    d_attn_own = d_resid.astype(BF)
    d_attn = ordered(d_attn_own, swap(d_attn_own), side)
    grad_out_w = matmul_tn(attended, d_attn)
    d_attended = matmul_nt(d_attn, w_output).astype(BF)
    d_qkv = attend_back(qkv, attended, lse, d_attended)
    grad_qkv = matmul_tn(first, d_qkv)
    d_first = matmul_nt(d_qkv, qkv_w)
    theirs = swap(rows_of(d_first, (1 - side) * tokens, tokens).astype(BF))
    d_first = rows_of(d_first, side * tokens, tokens) + theirs.astype(F32)
    d_source, grad_pre_gain, grad_pre_shift = jax.vjp(
        layer_norm, inputs.astype(F32), pre_gain, pre_shift
    )[1](d_first)
    grad_inputs = d_resid + d_source

    mixed = mix[:, 0:1] * dense + coef * collect(out_back)
    theirs = swap(rows_of(mixed, (1 - side) * tokens, tokens).astype(BF))
    output = (
        rows_of(resid, side * tokens, tokens)
        + rows_of(mixed, side * tokens, tokens)
        + theirs.astype(F32)
    ).astype(BF)

    def reduce_rows(value):
        return lax.psum_scatter(value, "ep", scatter_dimension=0, tiled=True)

    up_rows = reduce_rows(grad_up.astype(BF))
    down_rows = reduce_rows(
        jnp.concatenate(
            [
                grad_down.astype(BF).reshape(owners, -1, width),
                grad_out_w.astype(BF).reshape(owners, -1, width),
            ],
            1,
        ).reshape(-1, width)
    )
    vectors = jnp.stack([grad_pre_gain, grad_pre_shift, grad_mid_gain, grad_mid_shift], 1)
    extra = jnp.concatenate([vectors, grad_small], 1)
    last_rows = reduce_rows(jnp.concatenate([grad_qkv, extra], 1).astype(BF))
    small_rows = last_rows[:, 3 * half :]
    mine = last_rows.shape[0] // 2

    def trade(rows):
        return rows_of(rows, side * mine, mine), swap(rows_of(rows, (1 - side) * mine, mine))

    up_own, up_theirs = trade(up_rows)
    grad_up_out = ordered(up_own, up_theirs, side, 1).astype(F32)
    last_own, last_theirs = trade(last_rows)

    def split_qkv(rows):
        rows = rows[:, : 3 * half].reshape(mine, pairs, 3, LANES)
        return [rows[:, :, at].reshape(mine, half) for at in range(3)]

    qkv_outs = [
        ordered(a, b, side, 1).astype(F32)
        for a, b in zip(split_qkv(last_own), split_qkv(last_theirs))
    ]
    extra_out = last_own[:, 3 * half :].astype(F32) + last_theirs[:, 3 * half :].astype(F32)
    route = [(2 * j + s, owners * s + j) for j in range(owners) for s in range(2)]
    down_rows = lax.ppermute(down_rows, ("ep", "es"), route).astype(F32)
    per_down = hidden_half // owners
    return (
        output,
        grad_inputs,
        extra_out[:, 0],
        extra_out[:, 1],
        qkv_outs[0],
        qkv_outs[1],
        qkv_outs[2],
        down_rows[per_down:],
        extra_out[:, 2],
        extra_out[:, 3],
        grad_up_out,
        down_rows[:per_down],
        extra_out[:, 4 : 4 + experts],
        extra_out[:, 4 + experts :],
        grad_expert_up,
        grad_expert_down,
    )


def solution(mesh):
    placed = (
        P(("ep", "es"), None),
        P(("ep", "es"), None),
        P(("ep", "es"), None),
        P(),
        P(),
        P("es", None),
        P("es", None),
        P("es", None),
        P("es", None),
        P(),
        P(),
        P("es", None),
        P("es", None),
        P(),
        P(),
        P("ep", None, "es"),
        P("ep", "es", None),
    )
    return jax.shard_map(
        body,
        mesh=mesh,
        in_specs=placed,
        out_specs=(
            P(("ep", "es"), None),
            P(("ep", "es"), None),
            P(("ep", "es")),
            P(("ep", "es")),
            P(("ep", "es"), None),
            P(("ep", "es"), None),
            P(("ep", "es"), None),
            P(("ep", "es"), None),
            P(("ep", "es")),
            P(("ep", "es")),
            P(("ep", "es"), None),
            P(("ep", "es"), None),
            P(("ep", "es"), None),
            P(("ep", "es"), None),
            P("ep", None, "es"),
            P("ep", "es", None),
        ),
        check_vma=False,
    )
```

```python
import jax
import jax.numpy as jnp
from jax import lax
from jax.experimental import pallas as pl
from jax.experimental.pallas import tpu as pltpu
from jax.sharding import PartitionSpec as P

HEAD_DIM = 64
SCALE = HEAD_DIM ** (-0.5)
LANES = 128
QB = 256
BF = jnp.bfloat16
F32 = jnp.float32


def layer_norm(values, gain, shift):
    center = jnp.mean(values, axis=-1, keepdims=True)
    centred = values - center
    spread = jnp.mean(centred * centred, axis=-1, keepdims=True)
    return centred * lax.rsqrt(spread + 1e-05) * gain + shift


def gelu_tanh(values):
    return jax.nn.gelu(values, approximate=True)


def matmul(left, right):
    return jnp.dot(left, right, preferred_element_type=F32)


def matmul_nt(left, right):
    return lax.dot_general(left, right, (((1,), (1,)), ((), ())), preferred_element_type=F32)


def matmul_tn(left, right):
    return lax.dot_general(left, right, (((0,), (0,)), ((), ())), preferred_element_type=F32)


def swap(value):
    return lax.ppermute(value, "es", [(0, 1), (1, 0)])


def core_swap(value):
    size = lax.axis_size("ep")
    return lax.ppermute(value, "ep", [(i, i ^ 1) for i in range(size)])


def rows_of(value, start, count, axis=0):
    return lax.dynamic_slice_in_dim(value, start, count, axis)


bar = lax.optimization_barrier


def fetch(payload, core, after):
    half = payload.shape[0] // 2
    part, after = bar((rows_of(payload, core * half, half), after))
    got = swap(part)
    other = core_swap(got)
    first = core == 0
    whole = jnp.concatenate([jnp.where(first, got, other), jnp.where(first, other, got)], 0)
    return whole, got, after


def core_sum(blocks):
    core = lax.axis_index("ep") % 2
    blocks = blocks.reshape((-1, 2) + blocks.shape[1:])
    keep = lax.dynamic_index_in_dim(blocks, core, 1, keepdims=False)
    send = lax.dynamic_index_in_dim(blocks, 1 - core, 1, keepdims=False)
    return keep.astype(F32) + core_swap(send).astype(F32)


def ordered(own, other, side, axis=0):
    early = side == 0
    return jnp.concatenate(
        [jnp.where(early, own, other), jnp.where(early, other, own)], axis
    )


def head_masks():
    lane = lax.broadcasted_iota(jnp.int32, (1, LANES), 1)
    return (lane < HEAD_DIM, lane >= HEAD_DIM)


def attend_kernel(qkv_ref, out_ref, lse_ref):
    length = qkv_ref.shape[0]
    masks = head_masks()
    for start in range(0, length, QB):
        reach = start + QB
        query = qkv_ref[start:reach, 0:LANES] * SCALE
        keys = qkv_ref[0:reach, LANES : 2 * LANES]
        values = qkv_ref[0:reach, 2 * LANES :]
        row = lax.broadcasted_iota(jnp.int32, (QB, reach), 0) + start
        col = lax.broadcasted_iota(jnp.int32, (QB, reach), 1)
        outs, logs = [], []
        for mask in masks:
            scores = matmul_nt(jnp.where(mask, query, 0.0).astype(BF), keys)
            scores = jnp.where(col <= row, scores, -1e30)
            peak = jnp.max(scores, axis=-1, keepdims=True)
            expo = jnp.exp(scores - peak)
            total = jnp.sum(expo, axis=-1, keepdims=True)
            probs = (expo * (1.0 / total)).astype(BF)
            outs.append(matmul(probs, values))
            logs.append(peak + jnp.log(total))
        out_ref[start:reach, :] = jnp.where(masks[0], outs[0], outs[1]).astype(BF)
        lse_ref[start:reach, :] = jnp.where(masks[0], logs[0], logs[1])


def attend_back_kernel(qkv_ref, out_ref, lse_ref, grad_ref, dqkv_ref, dk_ref, dv_ref):
    length = qkv_ref.shape[0]
    masks = head_masks()
    for start in reversed(range(0, length, QB)):
        reach = start + QB
        query = qkv_ref[start:reach, 0:LANES] * SCALE
        keys = qkv_ref[0:reach, LANES : 2 * LANES]
        values = qkv_ref[0:reach, 2 * LANES :]
        grad = grad_ref[start:reach, :]
        weighed = grad.astype(F32) * out_ref[start:reach, :].astype(F32)
        row = lax.broadcasted_iota(jnp.int32, (QB, reach), 0) + start
        col = lax.broadcasted_iota(jnp.int32, (QB, reach), 1)
        dq, dk, dv = [], None, None
        for h, mask in enumerate(masks):
            q_h = jnp.where(mask, query, 0.0).astype(BF)
            g_h = jnp.where(mask, grad, 0.0).astype(BF)
            scores = matmul_nt(q_h, keys)
            lse = lse_ref[start:reach, h * HEAD_DIM : h * HEAD_DIM + 1]
            probs = jnp.where(col <= row, jnp.exp(scores - lse), 0.0)
            delta = jnp.sum(jnp.where(mask, weighed, 0.0), axis=-1, keepdims=True)
            d_scores = (probs * (matmul_nt(g_h, values) - delta)).astype(BF)
            dq.append(matmul(d_scores, keys))
            dk_h = matmul_tn(d_scores, q_h)
            dv_h = matmul_tn(probs.astype(BF), g_h)
            dk = dk_h if dk is None else dk + dk_h
            dv = dv_h if dv is None else dv + dv_h
        dqkv_ref[start:reach, 0:LANES] = (
            jnp.where(masks[0], dq[0], dq[1]) * SCALE
        ).astype(BF)
        if reach == length:
            dk_ref[...] = dk
            dv_ref[...] = dv
        else:
            dk_ref[0:reach, :] += dk
            dv_ref[0:reach, :] += dv
    dqkv_ref[:, LANES : 2 * LANES] = dk_ref[...].astype(BF)
    dqkv_ref[:, 2 * LANES :] = dv_ref[...].astype(BF)


def attend(qkv):
    length, columns = qkv.shape
    pairs = columns // (3 * LANES)
    wide = pl.BlockSpec((length, 3 * LANES), lambda h: (0, h))
    slim = pl.BlockSpec((length, LANES), lambda h: (0, h))
    return pl.pallas_call(
        attend_kernel,
        grid=(pairs,),
        in_specs=[wide],
        out_specs=[slim, slim],
        out_shape=[
            jax.ShapeDtypeStruct((length, pairs * LANES), BF),
            jax.ShapeDtypeStruct((length, pairs * LANES), F32),
        ],
        name="attend",
    )(qkv)


def attend_back(qkv, out, lse, grad):
    length, columns = qkv.shape
    pairs = columns // (3 * LANES)
    wide = pl.BlockSpec((length, 3 * LANES), lambda h: (0, h))
    slim = pl.BlockSpec((length, LANES), lambda h: (0, h))
    return pl.pallas_call(
        attend_back_kernel,
        grid=(pairs,),
        in_specs=[wide, slim, slim, slim],
        out_specs=wide,
        out_shape=jax.ShapeDtypeStruct((length, columns), BF),
        scratch_shapes=[pltpu.VMEM((length, LANES), F32), pltpu.VMEM((length, LANES), F32)],
        name="attend_back",
    )(qkv, out, lse, grad)


def pieces(value):
    high = lax.reduce_precision(value, 8, 7)
    rest = value - high
    mid = lax.reduce_precision(rest, 8, 7)
    return [high, mid, rest - mid]


def layer(
    inputs,
    grad_output,
    expert_choice,
    pre_gain,
    pre_shift,
    w_query,
    w_key,
    w_value,
    w_output,
    mid_gain,
    mid_shift,
    w_up,
    w_down,
    w_router,
    w_mix,
    expert_up,
    expert_down,
):
    tokens, width = inputs.shape
    owners = lax.axis_size("ep")
    experts = w_router.shape[1]
    capacity = max(2, 10 * tokens // (7 * owners))
    room = -(-(capacity + 3) // 16) * 16
    side = lax.axis_index("es")
    rank = lax.axis_index("ep")
    core = rank % 2
    half = w_query.shape[0]
    pairs = half // LANES
    hidden_half = w_down.shape[0]

    def pair_columns(at):
        parts = [
            rows_of(w, at * half, half, 1).reshape(half, pairs, 1, LANES)
            for w in (w_query, w_key, w_value)
        ]
        return jnp.concatenate(parts, 2).reshape(half, 3 * half)

    chosen = expert_choice[:, 0]
    onehot = (chosen[:, None] == jnp.arange(experts, dtype=jnp.int32)[None, :]).astype(jnp.int32)
    own_place = chosen * room + jnp.sum(onehot * jnp.cumsum(onehot, axis=0), axis=1) - 1
    slots = experts * room
    number = jnp.arange(slots, dtype=jnp.int32)

    inputs_other = swap(inputs)
    place_other = swap(own_place)
    qkv_other, qkv_got, grad_output = fetch(pair_columns(1 - side), core, grad_output)

    def exchange(rows):
        return lax.all_to_all(
            rows.reshape(owners, -1, width), "ep", split_axis=0, concat_axis=0, tiled=True
        )

    own_hit = (number[:, None] == own_place[None, :]).astype(BF)
    grad_arrived = exchange(matmul(own_hit, grad_output).astype(BF))

    output_other, output_got, qkv_got = fetch(w_output, core, qkv_got)
    up_other, up_got, output_got = fetch(
        rows_of(w_up, (1 - side) * hidden_half, hidden_half, 1), core, output_got
    )

    source = ordered(inputs, inputs_other, side).astype(F32)
    qkv_w = ordered(pair_columns(side), qkv_other, side)
    up_w = ordered(rows_of(w_up, side * hidden_half, hidden_half, 1), up_other, side)
    place = ordered(own_place, place_other, side)
    onehot = ((place // room)[:, None] == jnp.arange(experts, dtype=jnp.int32)[None, :])
    hit = number[None, :, None] == place.reshape(2, 1, tokens)
    placing = hit.astype(BF)

    def dispatch(rows):
        return jnp.einsum(
            "bst,btd->bsd", placing, rows.reshape(2, tokens, width), preferred_element_type=F32
        )

    def collect(arrived):
        rows = arrived.reshape(experts, 2, room, width)
        return jnp.einsum(
            "bst,sbd->btd",
            placing,
            rows.transpose(0, 2, 1, 3).reshape(slots, 2, width),
            preferred_element_type=F32,
        ).reshape(2 * tokens, width)

    pad_row = jnp.arange(room, dtype=jnp.int32)[None, None, :, None] - capacity

    def with_scalars(rows, scalars):
        wide = [
            jnp.pad(piece, ((0, 0), (0, 0), (0, width - room)))[:, :, None, :]
            for piece in pieces(scalars)
        ]
        for at, piece in enumerate(wide):
            rows = jnp.where(pad_row == at, piece, rows)
        return rows.astype(BF)

    def scalars_of(rows):
        spare = rows[:, :, capacity : capacity + 3, :room].astype(F32)
        return spare[:, :, 0] + spare[:, :, 1] + spare[:, :, 2]

    def to_owner(rows):
        return rows.reshape(2, owners, room, -1).transpose(1, 0, 2, 3)

    first = layer_norm(source, pre_gain, pre_shift).astype(BF)
    qkv = matmul(first, qkv_w).astype(BF)
    attended, lse = attend(qkv)
    attended, up_got = bar((attended, up_got))
    attended_other = swap(attended)
    grad_output, attended_other = bar((grad_output, attended_other))
    grad_other = swap(grad_output)
    grad_arrived, grad_other = bar((grad_arrived, grad_other))
    grad_slots = ordered(
        grad_arrived[:, None], swap(grad_arrived)[:, None], side, 1
    )
    upstream = ordered(grad_output, grad_other, side)
    resid = source + matmul(attended, w_output) + matmul(attended_other, output_other)
    second = layer_norm(resid, mid_gain, mid_shift).astype(BF)
    small_w = jnp.concatenate([w_router, w_mix], 1)
    logits = matmul(second, small_w)
    route_probs = jax.nn.softmax(logits[:, :experts], axis=-1)
    mask = onehot.astype(F32)
    gate = jnp.sum(route_probs * mask, axis=-1, keepdims=True)
    mix = jax.nn.softmax(logits[:, experts:], axis=-1)
    coef = mix[:, 1:2] * gate

    coef_slots = jnp.sum(
        jnp.where(hit, coef.reshape(2, 1, tokens), 0.0), axis=-1
    )
    sent = with_scalars(
        to_owner(dispatch(second)), coef_slots.reshape(2, owners, room).transpose(1, 0, 2)
    )
    arrived = exchange(sent)

    count = owners * 2 * room
    grad_there = grad_slots.reshape(count, width)
    up_pre = matmul(second, up_w)
    hidden = gelu_tanh(up_pre).astype(BF)
    dense = matmul(hidden, w_down)
    up32 = upstream.astype(F32)
    d_dense = (mix[:, 0:1] * up32).astype(BF)
    d_up = jax.vjp(gelu_tanh, up_pre)[1](matmul_nt(d_dense, w_down))[0].astype(BF)
    raw_hidden = matmul_nt(grad_there, expert_down[0])
    mixed = mix[:, 0:1] * dense
    mixed_theirs = swap(rows_of(mixed, (1 - side) * tokens, tokens).astype(BF))
    arrived, dense, d_up, raw_hidden = bar((arrived, dense, d_up, raw_hidden))

    coef_there = scalars_of(arrived.reshape(owners, 2, room, width)).reshape(count, 1)
    gathered = arrived.reshape(count, width)
    expert_pre = matmul(gathered, expert_up[0])
    expert_hidden = gelu_tanh(expert_pre).astype(BF)
    d_expert_pre = jax.vjp(gelu_tanh, expert_pre)[1](coef_there * raw_hidden)[0]
    d_expert_pre = d_expert_pre.astype(BF)
    along = jnp.sum(expert_hidden.astype(F32) * raw_hidden, axis=-1)
    d_slots = matmul_nt(d_expert_pre, expert_up[0])
    back_sent = with_scalars(
        d_slots.reshape(owners, 2, room, width), along.reshape(owners, 2, room)
    )
    back_sent, d_expert_pre, expert_hidden, d_up, d_dense = bar(
        (back_sent, d_expert_pre, expert_hidden, d_up, d_dense)
    )
    back = exchange(back_sent)
    expert_out = matmul(expert_hidden, expert_down[0]).reshape(owners, 2, room, width)
    out_theirs = lax.dynamic_index_in_dim(expert_out, 1 - side, 1, keepdims=False)
    out_mine = lax.dynamic_index_in_dim(expert_out, side, 1, keepdims=False)
    out_theirs = swap(out_theirs.astype(BF))
    expert_out = (out_mine + out_theirs.astype(F32)).astype(BF)
    d_routed = (coef_there * grad_there.astype(F32)).astype(BF)
    grad_expert_down = matmul_tn(expert_hidden, d_routed)
    grad_expert_up = matmul_tn(gathered, d_expert_pre)
    d_second = matmul_nt(d_up, up_w)
    grad_down = matmul_tn(hidden, d_dense).astype(BF)
    grad_up = [matmul_tn(second, part).astype(BF) for part in (d_up[:, :width], d_up[:, width:])]
    grad_ff = jnp.concatenate(
        [
            part.reshape(owners, -1, width)
            for part in grad_up + [grad_down]
        ],
        1,
    ).reshape(-1, width)
    back, expert_out, grad_expert_down, grad_expert_up, d_second, grad_ff = bar(
        (back, expert_out, grad_expert_down, grad_expert_up, d_second, grad_ff)
    )
    out_back = exchange(expert_out)

    back_rows = back.reshape(owners, 2, room, width)
    along_here = jnp.sum(
        jnp.where(
            hit, scalars_of(back_rows).transpose(1, 0, 2).reshape(2, slots, 1), 0.0
        ),
        axis=1,
    ).reshape(2 * tokens, 1)
    along_dense = jnp.sum(up32 * dense, axis=-1, keepdims=True)
    d_gate = mix[:, 1:2] * along_here
    d_both = jnp.concatenate([along_dense, gate * along_here], 1)
    d_route = route_probs * (mask * d_gate - gate * d_gate)
    d_mix = mix * (d_both - jnp.sum(mix * d_both, axis=-1, keepdims=True))
    d_small = jnp.concatenate([d_route, d_mix], 1).astype(BF)
    grad_small = matmul_tn(second, d_small)

    d_second = d_second + matmul_nt(d_small, small_w) + collect(back)
    theirs = swap(rows_of(d_second, (1 - side) * tokens, tokens).astype(BF))
    d_second = rows_of(d_second, side * tokens, tokens) + theirs.astype(F32)
    d_resid_mid, grad_mid_gain, grad_mid_shift = jax.vjp(
        layer_norm, rows_of(resid, side * tokens, tokens), mid_gain, mid_shift
    )[1](d_second)
    d_resid = grad_output.astype(F32) + d_resid_mid
    d_attn_own = d_resid.astype(BF)
    d_attn_other = swap(d_attn_own)
    d_attn = ordered(d_attn_own, d_attn_other, side)
    grad_out_w = matmul_tn(attended, d_attn).astype(BF)
    out_sums = core_sum(grad_out_w.reshape(owners, -1, width)).astype(BF)
    groups = [list(range(at, owners, 2)) for at in range(2)]
    out_rows = lax.all_to_all(out_sums, "ep", 0, 0, axis_index_groups=groups, tiled=True)
    out_rows = jnp.sum(out_rows.astype(F32), axis=0)
    d_attended = matmul_nt(d_attn, w_output).astype(BF)
    d_qkv = attend_back(qkv, attended, lse, d_attended)
    routed = matmul_tn(own_hit, out_back.reshape(slots, width))
    output = (
        rows_of(resid, side * tokens, tokens)
        + rows_of(mixed, side * tokens, tokens)
        + mixed_theirs.astype(F32)
        + rows_of(coef, side * tokens, tokens) * routed
    ).astype(BF)
    d_first = matmul_nt(d_qkv, qkv_w)
    theirs = swap(rows_of(d_first, (1 - side) * tokens, tokens).astype(BF))
    grad_pre_gain, grad_pre_shift = jax.vjp(
        lambda gain, shift: layer_norm(source, gain, shift), pre_gain, pre_shift
    )[1](d_first)
    grad_qkv = matmul_tn(first, d_qkv).astype(BF)
    d_first = rows_of(d_first, side * tokens, tokens) + theirs.astype(F32)
    d_source = jax.vjp(lambda v: layer_norm(v, pre_gain, pre_shift), inputs.astype(F32))[1](
        d_first
    )[0]
    grad_inputs = d_resid + d_source

    ff_rows = lax.psum_scatter(grad_ff, "ep", scatter_dimension=0, tiled=True)
    mine = width // (2 * owners)
    vectors = jnp.stack([grad_pre_gain, grad_pre_shift, grad_mid_gain, grad_mid_shift], 1)
    small = jnp.concatenate([vectors, grad_small], 1)
    count = small.shape[1]
    spare = [piece.astype(BF) for piece in pieces(core_sum(small.reshape(owners, 2 * mine, -1)))]
    columns = 3 * half
    last = jnp.concatenate(
        [core_sum(grad_qkv.reshape(owners, 2 * mine, -1)).astype(BF)]
        + spare
        + [jnp.zeros((owners // 2, 2 * mine, -3 * count % LANES), BF)],
        2,
    )
    groups = [
        [2 * i + s for i in range(at, owners, 2) for s in range(2)] for at in range(2)
    ]
    last = lax.all_to_all(
        last.reshape(owners, mine, -1),
        ("ep", "es"),
        0,
        0,
        axis_index_groups=groups,
        tiled=True,
    )
    last = jnp.sum(last.reshape(owners // 2, 2, mine, -1).astype(F32), axis=0)
    small_out = last[0, :, columns:] + last[1, :, columns:]
    small_out = jnp.sum(small_out[:, : 3 * count].reshape(mine, 3, count), axis=1)
    qkv_out = last[:, :, :columns].reshape(2, mine, pairs, 3, LANES)
    qkv_outs = [
        qkv_out[:, :, :, at].transpose(1, 0, 2, 3).reshape(mine, 2 * half) for at in range(3)
    ]

    def trade(rows):
        return rows_of(rows, side * mine, mine), swap(rows_of(rows, (1 - side) * mine, mine))

    up_count = 2 * mine
    up_rows = jnp.concatenate([ff_rows[:up_count], ff_rows[up_count : 2 * up_count]], 1)
    up_own, up_theirs = trade(up_rows)
    grad_up_out = ordered(up_own, up_theirs, side, 1).astype(F32)
    route = [(2 * j + s, owners * s + j) for j in range(owners) for s in range(2)]
    down_out = lax.ppermute(ff_rows[2 * up_count :], ("ep", "es"), route).astype(F32)
    output_out = lax.ppermute(out_rows.astype(BF), ("ep", "es"), route).astype(F32)
    return (
        output,
        grad_inputs,
        small_out[:, 0],
        small_out[:, 1],
        qkv_outs[0],
        qkv_outs[1],
        qkv_outs[2],
        output_out,
        small_out[:, 2],
        small_out[:, 3],
        grad_up_out,
        down_out,
        small_out[:, 4 : 4 + experts],
        small_out[:, 4 + experts :],
        grad_expert_up[None],
        grad_expert_down[None],
    )


def solution(mesh):
    placed = (
        P(("ep", "es"), None),
        P(("ep", "es"), None),
        P(("ep", "es"), None),
        P(),
        P(),
        P("es", None),
        P("es", None),
        P("es", None),
        P("es", None),
        P(),
        P(),
        P("es", None),
        P("es", None),
        P(),
        P(),
        P("ep", None, "es"),
        P("ep", "es", None),
    )
    return jax.shard_map(
        layer,
        mesh=mesh,
        in_specs=placed,
        out_specs=(
            P(("ep", "es"), None),
            P(("ep", "es"), None),
            P(("ep", "es")),
            P(("ep", "es")),
            P(("ep", "es"), None),
            P(("ep", "es"), None),
            P(("ep", "es"), None),
            P(("ep", "es"), None),
            P(("ep", "es")),
            P(("ep", "es")),
            P(("ep", "es"), None),
            P(("ep", "es"), None),
            P(("ep", "es"), None),
            P(("ep", "es"), None),
            P("ep", None, "es"),
            P("ep", "es", None),
        ),
        check_vma=False,
    )
```

```python
import jax
import jax.numpy as jnp
from jax import lax
from jax.experimental import pallas as pl
from jax.experimental.pallas import tpu as pltpu
from jax.sharding import PartitionSpec as P

HEAD_DIM = 64
SCALE = HEAD_DIM ** (-0.5)
LANES = 128
QB = 256
BF = jnp.bfloat16
F32 = jnp.float32


def layer_norm(values, gain, shift):
    center = jnp.mean(values, axis=-1, keepdims=True)
    centred = values - center
    spread = jnp.mean(centred * centred, axis=-1, keepdims=True)
    return centred * lax.rsqrt(spread + 1e-05) * gain + shift


def gelu_tanh(values):
    return jax.nn.gelu(values, approximate=True)


def matmul(left, right):
    return jnp.dot(left, right, preferred_element_type=F32)


def matmul_nt(left, right):
    return lax.dot_general(left, right, (((1,), (1,)), ((), ())), preferred_element_type=F32)


def matmul_tn(left, right):
    return lax.dot_general(left, right, (((0,), (0,)), ((), ())), preferred_element_type=F32)


def swap(value):
    return lax.ppermute(value, "es", [(0, 1), (1, 0)])


def core_swap(value):
    size = lax.axis_size("ep")
    return lax.ppermute(value, "ep", [(i, i ^ 1) for i in range(size)])


def rows_of(value, start, count, axis=0):
    return lax.dynamic_slice_in_dim(value, start, count, axis)


bar = lax.optimization_barrier


def fetch(payload, core, after):
    half = payload.shape[0] // 2
    part, after = bar((rows_of(payload, core * half, half), after))
    got = swap(part)
    other = core_swap(got)
    first = core == 0
    whole = jnp.concatenate([jnp.where(first, got, other), jnp.where(first, other, got)], 0)
    return whole, got, after


def core_sum(blocks):
    core = lax.axis_index("ep") % 2
    blocks = blocks.reshape((-1, 2) + blocks.shape[1:])
    keep = lax.dynamic_index_in_dim(blocks, core, 1, keepdims=False)
    send = lax.dynamic_index_in_dim(blocks, 1 - core, 1, keepdims=False)
    return keep.astype(F32) + core_swap(send).astype(F32)


def ordered(own, other, side, axis=0):
    early = side == 0
    return jnp.concatenate(
        [jnp.where(early, own, other), jnp.where(early, other, own)], axis
    )


def head_masks():
    lane = lax.broadcasted_iota(jnp.int32, (1, LANES), 1)
    return (lane < HEAD_DIM, lane >= HEAD_DIM)


def attend_kernel(qkv_ref, out_ref, lse_ref):
    length = qkv_ref.shape[0]
    masks = head_masks()
    for start in range(0, length, QB):
        reach = start + QB
        query = qkv_ref[start:reach, 0:LANES] * SCALE
        keys = qkv_ref[0:reach, LANES : 2 * LANES]
        values = qkv_ref[0:reach, 2 * LANES :]
        row = lax.broadcasted_iota(jnp.int32, (QB, reach), 0) + start
        col = lax.broadcasted_iota(jnp.int32, (QB, reach), 1)
        outs, logs = [], []
        for mask in masks:
            scores = matmul_nt(jnp.where(mask, query, 0.0).astype(BF), keys)
            scores = jnp.where(col <= row, scores, -1e30)
            peak = jnp.max(scores, axis=-1, keepdims=True)
            expo = jnp.exp(scores - peak)
            total = jnp.sum(expo, axis=-1, keepdims=True)
            probs = (expo * (1.0 / total)).astype(BF)
            outs.append(matmul(probs, values))
            logs.append(peak + jnp.log(total))
        out_ref[start:reach, :] = jnp.where(masks[0], outs[0], outs[1]).astype(BF)
        lse_ref[start:reach, :] = jnp.where(masks[0], logs[0], logs[1])


def attend_back_kernel(qkv_ref, out_ref, lse_ref, grad_ref, dqkv_ref, dk_ref, dv_ref):
    length = qkv_ref.shape[0]
    masks = head_masks()
    for start in reversed(range(0, length, QB)):
        reach = start + QB
        query = qkv_ref[start:reach, 0:LANES] * SCALE
        keys = qkv_ref[0:reach, LANES : 2 * LANES]
        values = qkv_ref[0:reach, 2 * LANES :]
        grad = grad_ref[start:reach, :]
        weighed = grad.astype(F32) * out_ref[start:reach, :].astype(F32)
        row = lax.broadcasted_iota(jnp.int32, (QB, reach), 0) + start
        col = lax.broadcasted_iota(jnp.int32, (QB, reach), 1)
        dq, dk, dv = [], None, None
        for h, mask in enumerate(masks):
            q_h = jnp.where(mask, query, 0.0).astype(BF)
            g_h = jnp.where(mask, grad, 0.0).astype(BF)
            scores = matmul_nt(q_h, keys)
            lse = lse_ref[start:reach, h * HEAD_DIM : h * HEAD_DIM + 1]
            probs = jnp.where(col <= row, jnp.exp(scores - lse), 0.0)
            delta = jnp.sum(jnp.where(mask, weighed, 0.0), axis=-1, keepdims=True)
            d_scores = (probs * (matmul_nt(g_h, values) - delta)).astype(BF)
            dq.append(matmul(d_scores, keys))
            dk_h = matmul_tn(d_scores, q_h)
            dv_h = matmul_tn(probs.astype(BF), g_h)
            dk = dk_h if dk is None else dk + dk_h
            dv = dv_h if dv is None else dv + dv_h
        dqkv_ref[start:reach, 0:LANES] = (
            jnp.where(masks[0], dq[0], dq[1]) * SCALE
        ).astype(BF)
        if reach == length:
            dk_ref[...] = dk
            dv_ref[...] = dv
        else:
            dk_ref[0:reach, :] += dk
            dv_ref[0:reach, :] += dv
    dqkv_ref[:, LANES : 2 * LANES] = dk_ref[...].astype(BF)
    dqkv_ref[:, 2 * LANES :] = dv_ref[...].astype(BF)


def attend(qkv, first, pairs):
    length = qkv.shape[0]
    wide = pl.BlockSpec((length, 3 * LANES), lambda h: (0, h + first))
    slim = pl.BlockSpec((length, LANES), lambda h: (0, h))
    return pl.pallas_call(
        attend_kernel,
        grid=(pairs,),
        in_specs=[wide],
        out_specs=[slim, slim],
        out_shape=[
            jax.ShapeDtypeStruct((length, pairs * LANES), BF),
            jax.ShapeDtypeStruct((length, pairs * LANES), F32),
        ],
        name="attend",
    )(qkv)


def attend_back(qkv, out, lse, grad):
    length, columns = qkv.shape
    pairs = columns // (3 * LANES)
    wide = pl.BlockSpec((length, 3 * LANES), lambda h: (0, h))
    slim = pl.BlockSpec((length, LANES), lambda h: (0, h))
    return pl.pallas_call(
        attend_back_kernel,
        grid=(pairs,),
        in_specs=[wide, slim, slim, slim],
        out_specs=wide,
        out_shape=jax.ShapeDtypeStruct((length, columns), BF),
        scratch_shapes=[pltpu.VMEM((length, LANES), F32), pltpu.VMEM((length, LANES), F32)],
        name="attend_back",
    )(qkv, out, lse, grad)


def pieces(value):
    high = lax.reduce_precision(value, 8, 7)
    rest = value - high
    mid = lax.reduce_precision(rest, 8, 7)
    return [high, mid, rest - mid]


def layer(
    inputs,
    grad_output,
    expert_choice,
    pre_gain,
    pre_shift,
    w_query,
    w_key,
    w_value,
    w_output,
    mid_gain,
    mid_shift,
    w_up,
    w_down,
    w_router,
    w_mix,
    expert_up,
    expert_down,
):
    tokens, width = inputs.shape
    owners = lax.axis_size("ep")
    experts = w_router.shape[1]
    capacity = max(2, 10 * tokens // (7 * owners))
    room = -(-(capacity + 3) // 16) * 16
    side = lax.axis_index("es")
    rank = lax.axis_index("ep")
    core = rank % 2
    half = w_query.shape[0]
    pairs = half // LANES
    hidden_half = w_down.shape[0]

    def paired(parts):
        rows = parts[0].shape[0]
        parts = [part.reshape(rows, pairs, 1, LANES) for part in parts]
        return jnp.concatenate(parts, 2).reshape(rows, 3 * half)

    def columns_of(rows, at):
        return [rows_of(rows(w), at * half, half, 1) for w in (w_query, w_key, w_value)]

    quarter = half // 2
    qkv_got = [
        swap(part) for part in columns_of(lambda w: rows_of(w, core * quarter, quarter), 1 - side)
    ]

    chosen = expert_choice[:, 0]
    onehot = (chosen[:, None] == jnp.arange(experts, dtype=jnp.int32)[None, :]).astype(jnp.int32)
    own_place = chosen * room + jnp.sum(onehot * jnp.cumsum(onehot, axis=0), axis=1) - 1
    slots = experts * room
    number = jnp.arange(slots, dtype=jnp.int32)

    inputs_other = swap(inputs)
    place_other = swap(own_place)
    qkv_got = paired(qkv_got)
    qkv_swapped = core_swap(qkv_got)
    lead = core == 0
    qkv_other = jnp.concatenate(
        [jnp.where(lead, qkv_got, qkv_swapped), jnp.where(lead, qkv_swapped, qkv_got)], 0
    )

    def exchange(rows):
        return lax.all_to_all(
            rows.reshape(owners, -1, width), "ep", split_axis=0, concat_axis=0, tiled=True
        )

    own_hit = (number[:, None] == own_place[None, :]).astype(BF)
    grad_arrived = exchange(matmul(own_hit, grad_output).astype(BF))

    output_other, _, inputs_other = fetch(w_output, core, inputs_other)
    up_other, _, inputs_other = fetch(
        rows_of(w_up, (1 - side) * hidden_half, hidden_half, 1), core, inputs_other
    )

    source = ordered(inputs, inputs_other, side).astype(F32)
    qkv_w = ordered(paired(columns_of(lambda w: w, side)), qkv_other, side)
    up_w = ordered(rows_of(w_up, side * hidden_half, hidden_half, 1), up_other, side)
    place = ordered(own_place, place_other, side)
    onehot = ((place // room)[:, None] == jnp.arange(experts, dtype=jnp.int32)[None, :])
    hit = number[None, :, None] == place.reshape(2, 1, tokens)
    placing = hit.astype(BF)

    def dispatch(rows):
        return jnp.einsum(
            "bst,btd->bsd", placing, rows.reshape(2, tokens, width), preferred_element_type=F32
        )

    def collect(arrived):
        rows = arrived.reshape(experts, 2, room, width)
        return jnp.einsum(
            "bst,sbd->btd",
            placing,
            rows.transpose(0, 2, 1, 3).reshape(slots, 2, width),
            preferred_element_type=F32,
        ).reshape(2 * tokens, width)

    pad_row = jnp.arange(room, dtype=jnp.int32)[None, None, :, None] - capacity

    def with_scalars(rows, scalars):
        wide = [
            jnp.pad(piece, ((0, 0), (0, 0), (0, width - room)))[:, :, None, :]
            for piece in pieces(scalars)
        ]
        for at, piece in enumerate(wide):
            rows = jnp.where(pad_row == at, piece, rows)
        return rows.astype(BF)

    def scalars_of(rows):
        spare = rows[:, :, capacity : capacity + 3, :room].astype(F32)
        return spare[:, :, 0] + spare[:, :, 1] + spare[:, :, 2]

    def to_owner(rows):
        return rows.reshape(2, owners, room, -1).transpose(1, 0, 2, 3)

    first = layer_norm(source, pre_gain, pre_shift).astype(BF)
    qkv = matmul(first, qkv_w).astype(BF)
    attended_a, lse_a = attend(qkv, 0, pairs // 2)
    other_a = swap(attended_a)
    attended_b, lse_b = attend(qkv, pairs // 2, pairs - pairs // 2)
    other_b = swap(attended_b)
    attended = jnp.concatenate([attended_a, attended_b], 1)
    lse = jnp.concatenate([lse_a, lse_b], 1)
    grad_output, other_b = bar((grad_output, other_b))
    grad_other = swap(grad_output)
    grad_arrived, grad_other = bar((grad_arrived, grad_other))
    grad_slots = ordered(
        grad_arrived[:, None], swap(grad_arrived)[:, None], side, 1
    )
    upstream = ordered(grad_output, grad_other, side)
    early = attended_a.shape[1]
    resid = source + matmul(attended, w_output) + matmul(other_a, output_other[:early])
    resid = resid + matmul(other_b, output_other[early:])
    second = layer_norm(resid, mid_gain, mid_shift).astype(BF)
    small_w = jnp.concatenate([w_router, w_mix], 1)
    logits = matmul(second, small_w)
    route_probs = jax.nn.softmax(logits[:, :experts], axis=-1)
    mask = onehot.astype(F32)
    gate = jnp.sum(route_probs * mask, axis=-1, keepdims=True)
    mix = jax.nn.softmax(logits[:, experts:], axis=-1)
    coef = mix[:, 1:2] * gate

    coef_slots = jnp.sum(
        jnp.where(hit, coef.reshape(2, 1, tokens), 0.0), axis=-1
    )
    sent = with_scalars(
        to_owner(dispatch(second)), coef_slots.reshape(2, owners, room).transpose(1, 0, 2)
    )
    arrived = exchange(sent)

    count = owners * 2 * room
    grad_there = grad_slots.reshape(count, width)
    up_pre = matmul(second, up_w)
    hidden = gelu_tanh(up_pre).astype(BF)
    dense = matmul(hidden, w_down)
    up32 = upstream.astype(F32)
    d_dense = (mix[:, 0:1] * up32).astype(BF)
    d_up = jax.vjp(gelu_tanh, up_pre)[1](matmul_nt(d_dense, w_down))[0].astype(BF)
    raw_hidden = matmul_nt(grad_there, expert_down[0])
    mixed = mix[:, 0:1] * dense
    mixed_theirs = swap(rows_of(mixed, (1 - side) * tokens, tokens).astype(BF))
    arrived, dense, d_up, raw_hidden = bar((arrived, dense, d_up, raw_hidden))

    coef_there = scalars_of(arrived.reshape(owners, 2, room, width)).reshape(count, 1)
    gathered = arrived.reshape(count, width)
    expert_pre = matmul(gathered, expert_up[0])
    expert_hidden = gelu_tanh(expert_pre).astype(BF)
    d_expert_pre = jax.vjp(gelu_tanh, expert_pre)[1](coef_there * raw_hidden)[0]
    d_expert_pre = d_expert_pre.astype(BF)
    along = jnp.sum(expert_hidden.astype(F32) * raw_hidden, axis=-1)
    d_slots = matmul_nt(d_expert_pre, expert_up[0])
    back_sent = with_scalars(
        d_slots.reshape(owners, 2, room, width), along.reshape(owners, 2, room)
    )
    back_sent, d_expert_pre, expert_hidden, d_up, d_dense = bar(
        (back_sent, d_expert_pre, expert_hidden, d_up, d_dense)
    )
    back = exchange(back_sent)
    expert_out = matmul(expert_hidden, expert_down[0]).reshape(owners, 2, room, width)
    out_theirs = lax.dynamic_index_in_dim(expert_out, 1 - side, 1, keepdims=False)
    out_mine = lax.dynamic_index_in_dim(expert_out, side, 1, keepdims=False)
    out_theirs = swap(out_theirs.astype(BF))
    expert_out = (out_mine + out_theirs.astype(F32)).astype(BF)
    d_routed = (coef_there * grad_there.astype(F32)).astype(BF)
    grad_expert_down = matmul_tn(expert_hidden, d_routed)
    grad_expert_up = matmul_tn(gathered, d_expert_pre)
    d_second = matmul_nt(d_up, up_w)
    grad_down = matmul_tn(hidden, d_dense).astype(BF)
    grad_up = [matmul_tn(second, part).astype(BF) for part in (d_up[:, :width], d_up[:, width:])]
    grad_ff = jnp.concatenate(
        [
            part.reshape(owners, -1, width)
            for part in grad_up + [grad_down]
        ],
        1,
    ).reshape(-1, width)
    back, expert_out, grad_expert_down, grad_expert_up, d_second, grad_ff = bar(
        (back, expert_out, grad_expert_down, grad_expert_up, d_second, grad_ff)
    )
    out_back = exchange(expert_out)

    back_rows = back.reshape(owners, 2, room, width)
    along_here = jnp.sum(
        jnp.where(
            hit, scalars_of(back_rows).transpose(1, 0, 2).reshape(2, slots, 1), 0.0
        ),
        axis=1,
    ).reshape(2 * tokens, 1)
    along_dense = jnp.sum(up32 * dense, axis=-1, keepdims=True)
    d_gate = mix[:, 1:2] * along_here
    d_both = jnp.concatenate([along_dense, gate * along_here], 1)
    d_route = route_probs * (mask * d_gate - gate * d_gate)
    d_mix = mix * (d_both - jnp.sum(mix * d_both, axis=-1, keepdims=True))
    d_small = jnp.concatenate([d_route, d_mix], 1).astype(BF)
    grad_small = matmul_tn(second, d_small)

    d_second = d_second + matmul_nt(d_small, small_w) + collect(back)
    theirs = swap(rows_of(d_second, (1 - side) * tokens, tokens).astype(BF))
    d_second = rows_of(d_second, side * tokens, tokens) + theirs.astype(F32)
    d_resid_mid, grad_mid_gain, grad_mid_shift = jax.vjp(
        layer_norm, rows_of(resid, side * tokens, tokens), mid_gain, mid_shift
    )[1](d_second)
    d_resid = grad_output.astype(F32) + d_resid_mid
    d_attn_own = d_resid.astype(BF)
    d_attn_other = swap(d_attn_own)
    d_attn = ordered(d_attn_own, d_attn_other, side)
    grad_out_w = matmul_tn(attended, d_attn).astype(BF)
    out_sums = core_sum(grad_out_w.reshape(owners, -1, width)).astype(BF)
    groups = [list(range(at, owners, 2)) for at in range(2)]
    out_rows = lax.all_to_all(out_sums, "ep", 0, 0, axis_index_groups=groups, tiled=True)
    out_rows = jnp.sum(out_rows.astype(F32), axis=0)
    d_attended = matmul_nt(d_attn, w_output).astype(BF)
    d_qkv = attend_back(qkv, attended, lse, d_attended)
    routed = matmul_tn(own_hit, out_back.reshape(slots, width))
    output = (
        rows_of(resid, side * tokens, tokens)
        + rows_of(mixed, side * tokens, tokens)
        + mixed_theirs.astype(F32)
        + rows_of(coef, side * tokens, tokens) * routed
    ).astype(BF)
    d_first = matmul_nt(d_qkv, qkv_w)
    theirs = swap(rows_of(d_first, (1 - side) * tokens, tokens).astype(BF))
    grad_pre_gain, grad_pre_shift = jax.vjp(
        lambda gain, shift: layer_norm(source, gain, shift), pre_gain, pre_shift
    )[1](d_first)
    grad_qkv = matmul_tn(first, d_qkv).astype(BF)
    d_first = rows_of(d_first, side * tokens, tokens) + theirs.astype(F32)
    d_source = jax.vjp(lambda v: layer_norm(v, pre_gain, pre_shift), inputs.astype(F32))[1](
        d_first
    )[0]
    grad_inputs = d_resid + d_source

    ff_rows = lax.psum_scatter(grad_ff, "ep", scatter_dimension=0, tiled=True)
    mine = width // (2 * owners)
    vectors = jnp.stack([grad_pre_gain, grad_pre_shift, grad_mid_gain, grad_mid_shift], 1)
    small = jnp.concatenate([vectors, grad_small], 1)
    count = small.shape[1]
    spare = [piece.astype(BF) for piece in pieces(core_sum(small.reshape(owners, 2 * mine, -1)))]
    columns = 3 * half
    last = jnp.concatenate(
        [core_sum(grad_qkv.reshape(owners, 2 * mine, -1)).astype(BF)]
        + spare
        + [jnp.zeros((owners // 2, 2 * mine, -3 * count % LANES), BF)],
        2,
    )
    groups = [
        [2 * i + s for i in range(at, owners, 2) for s in range(2)] for at in range(2)
    ]
    last = lax.all_to_all(
        last.reshape(owners, mine, -1),
        ("ep", "es"),
        0,
        0,
        axis_index_groups=groups,
        tiled=True,
    )
    last = jnp.sum(last.reshape(owners // 2, 2, mine, -1).astype(F32), axis=0)
    small_out = last[0, :, columns:] + last[1, :, columns:]
    small_out = jnp.sum(small_out[:, : 3 * count].reshape(mine, 3, count), axis=1)
    qkv_out = last[:, :, :columns].reshape(2, mine, pairs, 3, LANES)
    qkv_outs = [
        qkv_out[:, :, :, at].transpose(1, 0, 2, 3).reshape(mine, 2 * half) for at in range(3)
    ]

    def trade(rows):
        return rows_of(rows, side * mine, mine), swap(rows_of(rows, (1 - side) * mine, mine))

    up_count = 2 * mine
    up_rows = jnp.concatenate([ff_rows[:up_count], ff_rows[up_count : 2 * up_count]], 1)
    up_own, up_theirs = trade(up_rows)
    grad_up_out = ordered(up_own, up_theirs, side, 1).astype(F32)
    route = [(2 * j + s, owners * s + j) for j in range(owners) for s in range(2)]
    down_out = lax.ppermute(ff_rows[2 * up_count :], ("ep", "es"), route).astype(F32)
    output_out = lax.ppermute(out_rows.astype(BF), ("ep", "es"), route).astype(F32)
    return (
        output,
        grad_inputs,
        small_out[:, 0],
        small_out[:, 1],
        qkv_outs[0],
        qkv_outs[1],
        qkv_outs[2],
        output_out,
        small_out[:, 2],
        small_out[:, 3],
        grad_up_out,
        down_out,
        small_out[:, 4 : 4 + experts],
        small_out[:, 4 + experts :],
        grad_expert_up[None],
        grad_expert_down[None],
    )


def solution(mesh):
    placed = (
        P(("ep", "es"), None),
        P(("ep", "es"), None),
        P(("ep", "es"), None),
        P(),
        P(),
        P("es", None),
        P("es", None),
        P("es", None),
        P("es", None),
        P(),
        P(),
        P("es", None),
        P("es", None),
        P(),
        P(),
        P("ep", None, "es"),
        P("ep", "es", None),
    )
    return jax.shard_map(
        layer,
        mesh=mesh,
        in_specs=placed,
        out_specs=(
            P(("ep", "es"), None),
            P(("ep", "es"), None),
            P(("ep", "es")),
            P(("ep", "es")),
            P(("ep", "es"), None),
            P(("ep", "es"), None),
            P(("ep", "es"), None),
            P(("ep", "es"), None),
            P(("ep", "es")),
            P(("ep", "es")),
            P(("ep", "es"), None),
            P(("ep", "es"), None),
            P(("ep", "es"), None),
            P(("ep", "es"), None),
            P("ep", None, "es"),
            P("ep", "es", None),
        ),
        check_vma=False,
    )
```
